32 devices in a mesh: groups: 2 (over x), ctx: 8 (over z, y), head: 2 (over core).
Axes of the slice: x: 2, y: 2, z: 4, core: 2. Of those that a mesh axis runs over, the one named last changes fastest.
Arguments:
- query_nope: bfloat16 [32, 128, 128], P('groups', ('ctx', 'head')), parts along dimension 0, may hold values from -6 to 6
- query_rope: bfloat16 [32, 8192], P('groups', ('ctx', 'head')), parts along dimension 0, may hold values from -31 to 31
- key_absorb: bfloat16 [128, 128, 512], P(('ctx', 'head')), may hold values from -0.5 to 0.5
- value_absorb: bfloat16 [128, 512, 128], P(('ctx', 'head')), may hold values from -4 to 4
- output_weight: bfloat16 [16384, 7168], P(('ctx', 'head')), may hold values from -0.0625 to 0.0625
- latent_cache: bfloat16 [3584, 64, 576], P(('groups', 'ctx')), parts along dimension 0, may hold values from -4 to 4
- page_owner: int32 [3584], P(('groups', 'ctx')), parts along dimension 0, may hold values from -1 to 15, as said below
Outputs:
- layer_output: bfloat16 [32, 7168], P('groups', ('ctx', 'head')), parts along dimension 0
The draws below stay inside these ranges and needn't reach their ends.
There are 2 independent parts, one for each index of `groups`. The reference program is written for one: setup_inputs(seed, part) draws one part's arguments, and reference() takes and returns one part's arrays. A program takes and returns all parts, laid end to end along the dimension named above; an argument that names none is the same for every part. Nothing has to cross between parts.
Inputs may be any that keep to these rules, and one draw needn't show every extreme that they name: `page_owner`: a slot's request, or -1 for an unused slot; every request owns at least one slot; every index of ctx has an eighth of its 224 slots or more in use, and some index has all 224 in use.
All inputs are finite; a program needn't handle non-finite values.
Results may differ from the reference program's by a relative error of at most 0.03.
Values may be sent and summed in bfloat16 or wider, within the bound.
A program may use at most 128 MiB of HBM per device.

```python
import jax
import jax.numpy as jnp
from jax import lax

D = 7168
H = 128
DN = 128
DR = 64
LAT = 512
DV = 128
PAGE = 64
BLOCK_PAGES = 8
R = 16
PAGES_DEV = 224
POOL = 1792
KV = 576


def load_pattern():
    device_count = POOL // PAGES_DEV
    lowest = PAGES_DEV // 8
    spread = max(device_count - 1, 1)
    return [lowest + (PAGES_DEV - lowest) * device * device // (spread * spread) for device in range(device_count)]


def page_layout(key):
    pattern = load_pattern()
    filled = sum(pattern)
    device_count = len(pattern)
    shuffled = jax.random.permutation(jax.random.fold_in(key, 11), device_count)
    device_load = jnp.array(pattern, jnp.int32)[shuffled]
    slot_ids = jnp.arange(POOL, dtype=jnp.int32)
    in_use = slot_ids % PAGES_DEV < device_load[slot_ids // PAGES_DEV]
    ranked = jnp.clip(jnp.cumsum(in_use.astype(jnp.int32)) - 1, 0, filled - 1)
    logical = jax.random.permutation(jax.random.fold_in(key, 13), filled).astype(jnp.int32)[ranked]
    boundary = jnp.sort(jax.random.permutation(jax.random.fold_in(key, 12), filled - 1).astype(jnp.int32)[:R - 1] + 1)
    owners = jnp.sum((logical[:, None] >= boundary[None, :]).astype(jnp.int32), axis=1)
    return jnp.where(in_use, owners, -1).astype(jnp.int32)


def draw_page_owner(key, part):
    owners = page_layout(key)
    return owners


def draw_latent_cache(key, part):
    latent = jax.random.truncated_normal(jax.random.fold_in(key, 21), -4.0, 4.0, (POOL, PAGE, LAT), jnp.float32)
    rope_part = jax.random.truncated_normal(jax.random.fold_in(key, 22), -4.0, 4.0, (POOL, PAGE, DR), jnp.float32)
    return jnp.concatenate([latent, rope_part], axis=2).astype(jnp.bfloat16)


def draw_query_rope(key, part):
    values = jax.random.truncated_normal(jax.random.fold_in(key, 32), -4.0, 4.0, (R, H, DR), jnp.float32)
    return values.reshape(R, H * DR).astype(jnp.bfloat16)


def strengthened(drawn, key, source, target, shards_of, factor):
    owner, partner = [(jnp.arange(drawn.shape[dim]) // (drawn.shape[dim] // shards_of)).reshape([-1 if axis == dim else 1 for axis in range(drawn.ndim)]) for dim in (source, target)]
    chosen = jax.random.permutation(key, shards_of)[partner]
    strong = (owner == chosen) | (owner == (partner + shards_of // 2) % shards_of)
    return jnp.where(strong, factor * drawn, drawn)


def block_scale(own_key, shape, cuts, low, high):
    factor_of, own = 1.0, jax.random.fold_in(own_key, 6)
    for dim, blocks in cuts:
        heights = jnp.exp(jax.random.uniform(jax.random.fold_in(own, dim), (blocks,), jnp.float32, low / len(cuts), high / len(cuts)))
        factor_of = factor_of * jnp.repeat(heights, shape[dim] // blocks).reshape([-1 if axis == dim else 1 for axis in range(len(shape))])
    return factor_of


def normal_values(own_key, extent, scale, bound, split=(), kind=jnp.bfloat16):
    values = jax.random.normal(own_key, extent, jnp.float32) * scale
    if len(split) > 0:
        values = block_scale(own_key, extent, split, -0.22, 0.18) * values
    return jnp.clip(values, min=-bound, max=bound).astype(kind)


def noise_with(rng, dims, scale, limit, cuts, heavy, held_as=jnp.bfloat16):
    values = scale * jax.random.normal(rng, dims, jnp.float32)
    if cuts:
        values = values * block_scale(rng, dims, cuts, -0.22, 0.18)
    return jnp.clip(strengthened(values, jax.random.fold_in(rng, 3), *heavy), -limit, limit).astype(held_as)


def setup_inputs(seed: int = 0, part: int = 0) -> dict:
    keys = jax.random.split(jax.random.key(seed), 8)
    own_keys = jax.random.split(jax.random.fold_in(keys[7], part), 8)
    query_nope = normal_values(own_keys[0], (R, H, DN), 1.0, 6.0, ((1, 16),))
    query_rope = draw_query_rope(jax.random.fold_in(jax.random.fold_in(keys[7], part), 71), part)
    key_absorb = normal_values(keys[2], (H, DN, LAT), DN ** -0.5, 0.5, ((0, 16),))
    value_absorb = normal_values(keys[3], (H, LAT, DV), 0.7, 4.0, ((0, 16),))
    output_weight = noise_with(keys[4], (H * DV, D), (H * DV) ** -0.5, 0.0625, ((0, 16),), (0, 1, 16, 2.0))
    latent_cache = draw_latent_cache(jax.random.fold_in(jax.random.fold_in(keys[7], part), 71), part)
    page_owner = draw_page_owner(jax.random.fold_in(jax.random.fold_in(keys[7], part), 71), part)
    return {"query_nope": query_nope, "query_rope": query_rope, "key_absorb": key_absorb, "value_absorb": value_absorb, "output_weight": output_weight, "latent_cache": latent_cache, "page_owner": page_owner}


masked_score = -1.0e30
highest = lax.Precision.HIGHEST


def reference(query_nope, query_rope, key_absorb, value_absorb, output_weight, latent_cache, page_owner):
    score_scale = (DN + DR) ** -0.5
    query_latent = jnp.einsum("rhn,hnl->rhl", query_nope.astype(jnp.float32), key_absorb.astype(jnp.float32), precision=highest).astype(jnp.bfloat16)
    query_full = jnp.concatenate([query_latent, query_rope.reshape(R, H, DR)], axis=2)
    block_count = POOL // BLOCK_PAGES
    cache_blocks = latent_cache.reshape(block_count, BLOCK_PAGES, PAGE, KV)
    owner_blocks = page_owner.reshape(block_count, BLOCK_PAGES)

    def score_block(inputs):
        page_rows, owner_ids = inputs
        page_query = query_full[jnp.clip(owner_ids, 0, R - 1)]
        scores = jnp.einsum("ptk,phk->pth", page_rows.astype(jnp.float32), page_query.astype(jnp.float32), precision=highest) * score_scale
        return jnp.where((owner_ids >= 0)[:, None, None], scores, masked_score)

    block_scores = lax.map(score_block, (cache_blocks, owner_blocks))
    page_max = jnp.max(block_scores, axis=2).reshape(POOL, H)
    owner_hot = page_owner[:, None] == jnp.arange(R, dtype=jnp.int32)[None, :]
    row_max = jnp.max(jnp.where(owner_hot[:, :, None], page_max[:, None, :], masked_score), axis=0)

    def sum_block(state, inputs):
        running_sum, running_total = state
        page_rows, owner_ids, scores = inputs
        onehot = (owner_ids[:, None] == jnp.arange(R, dtype=jnp.int32)[None, :]).astype(jnp.float32)
        offset = row_max[jnp.clip(owner_ids, 0, R - 1)]
        weights = jnp.where((owner_ids >= 0)[:, None, None], jnp.exp(scores - offset[:, None, :]), 0.0)
        weight_half = weights.astype(jnp.bfloat16).astype(jnp.float32)
        page_out = jnp.einsum("pth,ptl->phl", weight_half, page_rows[:, :, :LAT].astype(jnp.float32), precision=highest)
        running_sum = running_sum + jnp.einsum("pr,phl->rhl", onehot, page_out, precision=highest)
        running_total = running_total + jnp.einsum("pr,ph->rh", onehot, jnp.sum(weights, axis=1), precision=highest)
        return (running_sum, running_total), None

    start_state = (jnp.zeros((R, H, LAT), jnp.float32), jnp.zeros((R, H), jnp.float32))
    (latent_sum, total), _ = lax.scan(sum_block, start_state, (cache_blocks, owner_blocks, block_scores))
    attended = (latent_sum / total[:, :, None]).astype(jnp.bfloat16)
    head_out = jnp.einsum("rhl,hlv->rhv", attended.astype(jnp.float32), value_absorb.astype(jnp.float32), precision=highest).astype(jnp.bfloat16)
    return jnp.dot(head_out.reshape(R, H * DV), output_weight, preferred_element_type=jnp.float32).astype(jnp.bfloat16)
```

```python
import functools

import jax
import jax.numpy as jnp
from jax import lax
from jax.experimental import pallas as pl
from jax.experimental.pallas import tpu as pltpu
from jax.sharding import PartitionSpec as P

F32 = jnp.float32
BF16 = jnp.bfloat16


def dot_nt(a, b):
    return lax.dot_general(a, b, (((1,), (1,)), ((), ())), preferred_element_type=F32)


def attention_kernel(heads_here, group, score_scale, owner_ref, q_ref, cache_ref, sum_ref, stat_ref,
                     pages, query, scores, peak, total, acc, sems):
    ctx = q_ref.shape[0]
    slots, heads, _ = acc.shape
    requests = slots - 1
    page_count, page_len, _ = pages.shape
    latent = acc.shape[2]
    chunks = sems.shape[0]
    chunk = page_count // chunks

    def fetch(i):
        window = pl.ds(i * chunk, chunk)
        return pltpu.make_async_copy(cache_ref.at[window], pages.at[window], sems.at[i])

    for i in range(chunks):
        fetch(i).start()
    for r in range(requests):
        rows = [q_ref[c, r * heads_here:(r + 1) * heads_here, :].astype(F32) for c in range(ctx)]
        query[r] = jnp.concatenate(rows, axis=0).astype(BF16)
    peak[...] = jnp.full_like(peak, -1e30)
    total[...] = jnp.zeros_like(total)
    acc[...] = jnp.zeros_like(acc)

    def score_group(base):
        found = []
        for j in range(group):
            owner = owner_ref[base + j]
            found.append(dot_nt(query[jnp.minimum(owner, requests - 1)], pages[base + j]) * score_scale)
        for j in range(group):
            owner = owner_ref[base + j]
            scores[base + j] = found[j]
            peak[owner] = jnp.maximum(peak[owner], found[j])

    @pl.loop(0, chunks)
    def _(i):
        fetch(i).wait()

        @pl.loop(0, chunk // group)
        def _(g):
            score_group(i * chunk + g * group)

    for r in range(slots):
        peak[r] = jnp.broadcast_to(jnp.max(peak[r], axis=1, keepdims=True), peak.shape[1:])

    @pl.loop(0, page_count // group)
    def _(g):
        base = g * group
        parts = []
        for j in range(group):
            owner = owner_ref[base + j]
            weight = jnp.exp(scores[base + j] - peak[owner])
            total[owner] = total[owner] + weight
            parts.append(jnp.dot(weight.astype(BF16), pages[base + j, :, :latent], preferred_element_type=F32))
        for j in range(group):
            owner = owner_ref[base + j]
            acc[owner] = acc[owner] + parts[j]

    lane = lax.broadcasted_iota(jnp.int32, stat_ref.shape, 1)
    stats = jnp.zeros(stat_ref.shape, F32)
    for r in range(requests):
        stats = jnp.where(lane == r, jnp.max(peak[r], axis=1, keepdims=True), stats)
        stats = jnp.where(lane == requests + r, jnp.sum(total[r], axis=1, keepdims=True), stats)
    stat_ref[...] = stats
    for c in range(ctx):
        part = acc[:requests, c * heads_here:(c + 1) * heads_here, :]
        sum_ref[c] = part.reshape(requests * heads_here, latent).astype(BF16)


def attention(gathered, cache, owners, requests, heads_here, latent, score_scale):
    ctx, _, entry = gathered.shape
    page_count, page_len, _ = cache.shape
    heads = ctx * heads_here
    chunks = next(n for n in (14, 8, 7, 4, 2, 1) if page_count % n == 0)
    group = next(n for n in (8, 4, 2, 1) if (page_count // chunks) % n == 0)
    return pl.pallas_call(
        functools.partial(attention_kernel, heads_here, group, score_scale),
        grid_spec=pltpu.PrefetchScalarGridSpec(
            num_scalar_prefetch=1,
            grid=(1,),
            in_specs=[
                pl.BlockSpec(gathered.shape, lambda i, o: (0, 0, 0), pipeline_mode=pl.Buffered(1)),
                pl.BlockSpec(memory_space=pl.ANY),
            ],
            out_specs=[
                pl.BlockSpec((ctx, requests * heads_here, latent), lambda i, o: (0, 0, 0), pipeline_mode=pl.Buffered(1)),
                pl.BlockSpec((heads, 128), lambda i, o: (0, 0), pipeline_mode=pl.Buffered(1)),
            ],
            scratch_shapes=[
                pltpu.VMEM((page_count, page_len, entry), BF16),
                pltpu.VMEM((requests, heads, entry), BF16),
                pltpu.VMEM((page_count, heads, page_len), F32),
                pltpu.VMEM((requests + 1, heads, page_len), F32),
                pltpu.VMEM((requests + 1, heads, page_len), F32),
                pltpu.VMEM((requests + 1, heads, latent), F32),
                pltpu.SemaphoreType.DMA((chunks,)),
            ],
        ),
        out_shape=[
            jax.ShapeDtypeStruct((ctx, requests * heads_here, latent), BF16),
            jax.ShapeDtypeStruct((heads, 128), F32),
        ],
        compiler_params=pltpu.CompilerParams(vmem_limit_bytes=48 << 20),
    )(owners, gathered, cache)


def body(query_nope, query_rope, key_absorb, value_absorb, output_weight, latent_cache, page_owner):
    requests, heads_here, nope_size = query_nope.shape
    latent_size = key_absorb.shape[2]
    rope_size = query_rope.shape[1] // heads_here
    score_scale = (nope_size + rope_size) ** (-0.5)
    query_latent = jnp.einsum(
        "rhn,hnl->rhl", query_nope, key_absorb, preferred_element_type=F32
    ).astype(BF16)
    query_mine = jnp.concatenate(
        [query_latent, query_rope.reshape(requests, heads_here, rope_size)], axis=2
    ).reshape(requests * heads_here, -1)
    gathered = lax.all_gather(query_mine, "ctx", axis=0, tiled=False)
    owners = jnp.where(page_owner < 0, requests, page_owner)
    sums, stats = attention(gathered, latent_cache, owners, requests, heads_here, latent_size, score_scale)
    ctx = gathered.shape[0]
    got_sum = lax.all_to_all(sums, "ctx", split_axis=0, concat_axis=0, tiled=True).reshape(
        ctx, requests, heads_here, latent_size).astype(F32)
    got_stat = lax.all_to_all(
        stats.reshape(ctx, heads_here, -1), "ctx", split_axis=0, concat_axis=0, tiled=True)
    got_max = got_stat[:, :, :requests].transpose(0, 2, 1)
    got_total = got_stat[:, :, requests:2 * requests].transpose(0, 2, 1)
    top_max = jnp.max(got_max, axis=0)
    factor = jnp.exp(got_max - top_max[None])
    mine_total = jnp.sum(factor * got_total, axis=0)
    mine_sum = jnp.sum(factor[..., None] * got_sum, axis=0)
    attended = (mine_sum / mine_total[..., None]).astype(BF16)
    head_out = jnp.einsum(
        "rhl,hlv->rhv", attended, value_absorb, preferred_element_type=F32
    ).astype(BF16)
    partial_out = jnp.dot(
        head_out.reshape(requests, -1), output_weight, preferred_element_type=F32
    )
    return lax.psum_scatter(
        partial_out.astype(BF16), ("ctx", "head"), scatter_dimension=1, tiled=True
    )


def solution(mesh):
    return jax.shard_map(
        body,
        mesh=mesh,
        in_specs=(
            P("groups", ("ctx", "head"), None),
            P("groups", ("ctx", "head")),
            P(("ctx", "head"), None, None),
            P(("ctx", "head"), None, None),
            P(("ctx", "head"), None),
            P(("groups", "ctx"), None, None),
            P(("groups", "ctx")),
        ),
        out_specs=P("groups", ("ctx", "head")),
        check_vma=False,
    )
```

```python
import functools

import jax
import jax.numpy as jnp
from jax import lax
from jax.experimental import pallas as pl
from jax.experimental.pallas import tpu as pltpu
from jax.sharding import PartitionSpec as P

F32 = jnp.float32
BF16 = jnp.bfloat16


def dot_nt(a, b):
    return lax.dot_general(a, b, (((1,), (1,)), ((), ())), preferred_element_type=F32)


def attention_kernel(heads_here, group, score_scale, owner_ref, q_ref, cache_ref, sum_ref, stat_ref,
                     pages, query, scores, peak, total, acc, sems):
    ctx = q_ref.shape[0]
    slots, heads, _ = acc.shape
    requests = slots - 1
    page_count, page_len, _ = pages.shape
    latent = acc.shape[2]
    chunks = sems.shape[0]
    chunk = page_count // chunks

    def fetch(i):
        window = pl.ds(i * chunk, chunk)
        return pltpu.make_async_copy(cache_ref.at[window], pages.at[window], sems.at[i])

    for i in range(chunks):
        fetch(i).start()
    for r in range(requests):
        rows = [q_ref[c, r * heads_here:(r + 1) * heads_here, :].astype(F32) for c in range(ctx)]
        query[r] = jnp.concatenate(rows, axis=0).astype(BF16)
    peak[...] = jnp.full_like(peak, -1e30)
    total[...] = jnp.zeros_like(total)
    acc[...] = jnp.zeros_like(acc)

    def score_group(base):
        found = []
        for j in range(group):
            owner = owner_ref[base + j]
            found.append(dot_nt(query[jnp.minimum(owner, requests - 1)], pages[base + j]) * score_scale)
        for j in range(group):
            owner = owner_ref[base + j]
            scores[base + j] = found[j]
            peak[owner] = jnp.maximum(peak[owner], found[j])

    @pl.loop(0, chunks)
    def _(i):
        fetch(i).wait()

        @pl.loop(0, chunk // group)
        def _(g):
            score_group(i * chunk + g * group)

    for r in range(slots):
        peak[r] = jnp.broadcast_to(jnp.max(peak[r], axis=1, keepdims=True), peak.shape[1:])

    @pl.loop(0, page_count // group)
    def _(g):
        base = g * group
        parts = []
        for j in range(group):
            owner = owner_ref[base + j]
            weight = jnp.exp(scores[base + j] - peak[owner])
            total[owner] = total[owner] + weight
            parts.append(jnp.dot(weight.astype(BF16), pages[base + j, :, :latent], preferred_element_type=F32))
        for j in range(group):
            owner = owner_ref[base + j]
            acc[owner] = acc[owner] + parts[j]

    lane = lax.broadcasted_iota(jnp.int32, (heads, stat_ref.shape[-1]), 1)
    top = jnp.zeros(lane.shape, F32)
    norm = jnp.zeros(lane.shape, F32)
    for r in range(requests):
        top = jnp.where(lane == r, jnp.max(peak[r], axis=1, keepdims=True), top)
        norm = jnp.where(lane == r, jnp.sum(total[r], axis=1, keepdims=True), norm)
    for c in range(ctx):
        rows = slice(c * heads_here, (c + 1) * heads_here)
        part = acc[:requests, rows, :]
        sum_ref[c % 2, c // 2] = part.reshape(requests * heads_here, latent).astype(BF16)
        stat_ref[c % 2, c // 2, 0] = top[rows]
        stat_ref[c % 2, c // 2, 1] = norm[rows]


def attention(gathered, cache, owners, requests, heads_here, latent, score_scale):
    ctx, _, entry = gathered.shape
    page_count, page_len, _ = cache.shape
    heads = ctx * heads_here
    sum_shape = (2, ctx // 2, requests * heads_here, latent)
    stat_shape = (2, ctx // 2, 2, heads_here, 128)
    chunks = next(n for n in (14, 8, 7, 4, 2, 1) if page_count % n == 0)
    group = next(n for n in (8, 4, 2, 1) if (page_count // chunks) % n == 0)
    return pl.pallas_call(
        functools.partial(attention_kernel, heads_here, group, score_scale),
        grid_spec=pltpu.PrefetchScalarGridSpec(
            num_scalar_prefetch=1,
            grid=(1,),
            in_specs=[
                pl.BlockSpec(gathered.shape, lambda i, o: (0, 0, 0), pipeline_mode=pl.Buffered(1)),
                pl.BlockSpec(memory_space=pl.ANY),
            ],
            out_specs=[
                pl.BlockSpec(sum_shape, lambda i, o: (0,) * 4, pipeline_mode=pl.Buffered(1)),
                pl.BlockSpec(stat_shape, lambda i, o: (0,) * 5, pipeline_mode=pl.Buffered(1)),
            ],
            scratch_shapes=[
                pltpu.VMEM((page_count, page_len, entry), BF16),
                pltpu.VMEM((requests, heads, entry), BF16),
                pltpu.VMEM((page_count, heads, page_len), F32),
                pltpu.VMEM((requests + 1, heads, page_len), F32),
                pltpu.VMEM((requests + 1, heads, page_len), F32),
                pltpu.VMEM((requests + 1, heads, latent), F32),
                pltpu.SemaphoreType.DMA((chunks,)),
            ],
        ),
        out_shape=[
            jax.ShapeDtypeStruct(sum_shape, BF16),
            jax.ShapeDtypeStruct(stat_shape, F32),
        ],
        compiler_params=pltpu.CompilerParams(vmem_limit_bytes=48 << 20),
    )(owners, gathered, cache)


def remote(src, dst, send_sem, recv_sem, where):
    return pltpu.make_async_remote_copy(
        src_ref=src, dst_ref=dst, send_sem=send_sem, recv_sem=recv_sem,
        device_id=where, device_id_type=pl.DeviceIdType.MESH)


def gather_kernel(nz, nope_ref, rope_ref, key_ref, out_ref, wide, rows, mine,
                  y_send, y_recv, up_send, up_recv, down_send, down_recv):
    requests, heads_here, _ = nope_ref.shape
    latent = key_ref.shape[2]
    rope = rope_ref.shape[1] // heads_here
    me = lax.axis_index("ctx")
    z, y = me // 2, me % 2
    partner = {"ctx": z * 2 + 1 - y}
    above, below = {"ctx": me + 2}, {"ctx": me - 2}
    has_above, has_below = z + 1 < nz, z > 0

    barrier = pltpu.get_barrier_semaphore()
    pl.semaphore_signal(barrier, inc=1, device_id=partner, device_id_type=pl.DeviceIdType.MESH)

    @pl.when(has_above)
    def _():
        pl.semaphore_signal(barrier, inc=1, device_id=above, device_id_type=pl.DeviceIdType.MESH)

    @pl.when(has_below)
    def _():
        pl.semaphore_signal(barrier, inc=1, device_id=below, device_id_type=pl.DeviceIdType.MESH)

    wide[...] = nope_ref[...].astype(F32)
    for h in range(heads_here):
        rows[:, h, :latent] = jnp.dot(wide[:, h, :].astype(BF16), key_ref[h], preferred_element_type=F32)
        rows[:, h, latent:] = rope_ref[:, h * rope:(h + 1) * rope].astype(F32)
    value = rows[...].reshape(requests * heads_here, latent + rope).astype(BF16)
    mine[...] = value
    out_ref[me] = value

    pl.semaphore_wait(barrier, 1 + has_above.astype(jnp.int32) + has_below.astype(jnp.int32))

    def across(origin, src):
        slot = out_ref.at[origin * 2 + y]
        return remote(slot if src is None else src, slot, y_send.at[origin], y_recv.at[origin], partner)

    def upward(step, src=None):
        slot = out_ref.at[me - 2 * step]
        return remote(slot if src is None else src, slot, up_send.at[step], up_recv.at[step], above)

    def downward(step, src=None):
        slot = out_ref.at[me + 2 * step]
        return remote(slot if src is None else src, slot, down_send.at[step], down_recv.at[step], below)

    def arrival(slot, sem):
        return remote(slot, slot, sem, sem, partner)

    @pl.when(has_above)
    def _():
        upward(0, mine).start()

    @pl.when(has_below)
    def _():
        downward(0, mine).start()

    across(z, mine).start()
    for step in range(nz - 1):
        @pl.when(z - 1 - step >= 0)
        def _():
            arrival(out_ref.at[me - 2 * (step + 1)], up_recv.at[step]).wait_recv()
            if step + 1 < nz - 1:
                @pl.when(has_above)
                def _():
                    upward(step + 1).start()
            across(z - 1 - step, None).start()

        @pl.when(z + 1 + step < nz)
        def _():
            arrival(out_ref.at[me + 2 * (step + 1)], down_recv.at[step]).wait_recv()
            if step + 1 < nz - 1:
                @pl.when(has_below)
                def _():
                    downward(step + 1).start()
            across(z + 1 + step, None).start()

    for origin in range(nz):
        across(origin, mine).wait_send()
        arrival(out_ref.at[origin * 2 + 1 - y], y_recv.at[origin]).wait_recv()
    for step in range(nz - 1):
        @pl.when(has_above & (z - step >= 0))
        def _():
            upward(step, mine).wait_send()

        @pl.when(has_below & (z + step < nz))
        def _():
            downward(step, mine).wait_send()


def gather_queries(query_nope, query_rope, key_absorb, ctx):
    requests, heads_here, nope = query_nope.shape
    entry = key_absorb.shape[2] + query_rope.shape[1] // heads_here
    nz = ctx // 2
    vmem = pl.BlockSpec(memory_space=pltpu.VMEM)
    dma = pltpu.SemaphoreType.DMA
    return pl.pallas_call(
        functools.partial(gather_kernel, nz),
        out_shape=jax.ShapeDtypeStruct((ctx, requests * heads_here, entry), BF16),
        in_specs=[vmem] * 3,
        out_specs=vmem,
        scratch_shapes=[
            pltpu.VMEM(query_nope.shape, F32),
            pltpu.VMEM((requests, heads_here, entry), F32),
            pltpu.VMEM((requests * heads_here, entry), BF16),
            dma((nz,)), dma((nz,)), dma((nz,)), dma((nz,)), dma((nz,)), dma((nz,)),
        ],
        compiler_params=pltpu.CompilerParams(collective_id=0, has_side_effects=True, vmem_limit_bytes=16 << 20),
    )(query_nope, query_rope, key_absorb)


def project_kernel(ctx, sum_ref, stat_ref, value_ref, weight_ref, out_ref,
                   weight, y_sum, y_stat, c_sum, c_stat, z_sum, z_stat, wide,
                   h_keep, h_out, h_in, p_out, p_in,
                   w_sem, ys_send, ys_recv, yt_send, yt_recv, zs_send, zs_recv, zt_send, zt_recv,
                   h_send, h_recv, p_send, p_recv):
    nz = ctx // 2
    requests, half = out_ref.shape
    block = 2 * half
    heads_here = value_ref.shape[0]
    latent = value_ref.shape[1]
    me, core = lax.axis_index("ctx"), lax.axis_index("head")
    z, y = me // 2, me % 2
    partner, twin = {"ctx": z * 2 + 1 - y}, {"head": 1 - core}

    barrier = pltpu.get_barrier_semaphore()
    for k in range(1, ctx):
        pl.semaphore_signal(barrier, inc=1, device_id={"ctx": (me + k) % ctx}, device_id_type=pl.DeviceIdType.MESH)
    pl.semaphore_signal(barrier, inc=1, device_id=twin, device_id_type=pl.DeviceIdType.MESH)
    load = pltpu.make_async_copy(weight_ref, weight, w_sem)
    load.start()
    pl.semaphore_wait(barrier, ctx)

    stat_copy = remote(stat_ref.at[1 - y], y_stat, yt_send, yt_recv, partner)
    stat_copy.start()
    y_copies = []
    for k in range(nz):
        target = (z + 1 + k) % nz
        copy = remote(sum_ref.at[1 - y, target], y_sum.at[k], ys_send.at[k], ys_recv.at[k], partner)
        copy.start()
        y_copies.append(copy)
    stat_copy.wait_recv()

    def spread(factor):
        return jnp.concatenate([factor[:, r:r + 1] for r in range(requests)], axis=0)

    z_copies = []
    for k in range(nz):
        target = (z + 1 + k) % nz
        top_a, norm_a = stat_ref[y, target, 0], stat_ref[y, target, 1]
        top_b, norm_b = y_stat[target, 0], y_stat[target, 1]
        top = jnp.maximum(top_a, top_b)
        keep_a, keep_b = jnp.exp(top_a - top), jnp.exp(top_b - top)
        norm = keep_a * norm_a + keep_b * norm_b
        rows_a, rows_b = spread(keep_a), spread(keep_b)
        y_copies[k].wait_recv()
        both = rows_a * sum_ref[y, target].astype(F32) + rows_b * y_sum[k].astype(F32)
        if k < nz - 1:
            c_sum[k] = both.astype(BF16)
            c_stat[k, 0] = top
            c_stat[k, 1] = norm
            there = {"ctx": target * 2 + y}
            for copy in (
                remote(c_stat.at[k], z_stat.at[k], zt_send.at[k], zt_recv.at[k], there),
                remote(c_sum.at[k], z_sum.at[k], zs_send.at[k], zs_recv.at[k], there),
            ):
                copy.start()
                z_copies.append(copy)
    for copy in z_copies[0::2]:
        copy.wait_recv()
    highest = top
    for k in range(nz - 1):
        highest = jnp.maximum(highest, z_stat[k, 0])
    keep = jnp.exp(top - highest)
    all_norm = keep * norm
    factors = []
    for k in range(nz - 1):
        factors.append(jnp.exp(z_stat[k, 0] - highest))
        all_norm = all_norm + factors[k] * z_stat[k, 1]
    safe = jnp.where(all_norm > 0, all_norm, 1.0)
    total = spread(keep / safe) * both
    for k in range(nz - 1):
        z_copies[2 * k + 1].wait_recv()
        total = total + spread(factors[k] / safe) * z_sum[k].astype(F32)
    wide[...] = total.reshape(requests, heads_here, latent)
    outs = []
    for h in range(heads_here):
        outs.append(jnp.dot(wide[:, h, :].astype(BF16), value_ref[h], preferred_element_type=F32).astype(BF16))
    head_out = jnp.concatenate(outs, axis=1)
    load.wait()

    aligned = block % 128 == 0
    h_copies, p_copies = [], []

    def place(k):
        return (me + 1 + k) % ctx if aligned else k

    def forward(k):
        target = place(k)
        h_copies[k].wait_recv()
        merged = h_keep[k] + h_in[k]
        if aligned:
            p_out[k] = merged.astype(BF16)
            if k < ctx - 1:
                copy = remote(p_out.at[k], p_in.at[k], p_send.at[k], p_recv.at[k], {"ctx": target})
                copy.start()
                p_copies.append(copy)
        else:
            p_out[k] = merged.astype(BF16)

            @pl.when(target != me)
            def _():
                slot = (target - me + ctx - 1) % ctx
                remote(p_out.at[k], p_in.at[slot], p_send.at[slot], p_recv.at[slot], {"ctx": target}).start()

    for k in range(ctx):
        if aligned:
            columns = weight[:, pl.ds(pl.multiple_of(place(k) * block, 128), block)]
        else:
            columns = weight[:, k * block:(k + 1) * block]
        part = jnp.dot(head_out, columns, preferred_element_type=F32)
        low, high = part[:, :half], part[:, half:]
        h_keep[k] = jnp.where(core == 0, low, high)
        h_out[k] = jnp.where(core == 0, high, low)
        copy = remote(h_out.at[k], h_in.at[k], h_send.at[k], h_recv.at[k], twin)
        copy.start()
        h_copies.append(copy)
        if k > 0:
            forward(k - 1)
    forward(ctx - 1)
    if aligned:
        result = h_keep[ctx - 1] + h_in[ctx - 1]
    else:
        result = p_out[me].astype(F32)
    for k in range(ctx - 1):
        remote(p_out.at[k], p_in.at[k], p_send.at[k], p_recv.at[k], partner).wait_recv()
        result = result + p_in[k].astype(F32)
    out_ref[...] = result.astype(BF16)
    for k in range(ctx - 1):
        remote(p_out.at[k], p_in.at[k], p_send.at[k], p_recv.at[k], partner).wait_send()
    for copy in h_copies + z_copies + y_copies + [stat_copy]:
        copy.wait_send()


def project(sums, stats, value_absorb, output_weight, ctx):
    nz = ctx // 2
    _, _, rows, latent = sums.shape
    heads_here = value_absorb.shape[0]
    requests = rows // heads_here
    half = output_weight.shape[1] // (2 * ctx)
    vmem = pl.BlockSpec(memory_space=pltpu.VMEM)
    dma = pltpu.SemaphoreType.DMA
    stat_tail = stats.shape[2:]
    return pl.pallas_call(
        functools.partial(project_kernel, ctx),
        out_shape=jax.ShapeDtypeStruct((requests, half), BF16),
        in_specs=[vmem, vmem, vmem, pl.BlockSpec(memory_space=pl.ANY)],
        out_specs=vmem,
        scratch_shapes=[
            pltpu.VMEM(output_weight.shape, BF16),
            pltpu.VMEM((nz, rows, latent), BF16),
            pltpu.VMEM((nz,) + stat_tail, F32),
            pltpu.VMEM((nz - 1, rows, latent), BF16),
            pltpu.VMEM((nz - 1,) + stat_tail, F32),
            pltpu.VMEM((nz - 1, rows, latent), BF16),
            pltpu.VMEM((nz - 1,) + stat_tail, F32),
            pltpu.VMEM((requests, heads_here, latent), F32),
            pltpu.VMEM((ctx, requests, half), F32),
            pltpu.VMEM((ctx, requests, half), F32),
            pltpu.VMEM((ctx, requests, half), F32),
            pltpu.VMEM((ctx, requests, half), BF16),
            pltpu.VMEM((ctx - 1, requests, half), BF16),
            dma, dma((nz,)), dma((nz,)), dma, dma,
            dma((nz - 1,)), dma((nz - 1,)), dma((nz - 1,)), dma((nz - 1,)),
            dma((ctx,)), dma((ctx,)), dma((ctx - 1,)), dma((ctx - 1,)),
        ],
        compiler_params=pltpu.CompilerParams(collective_id=1, has_side_effects=True, vmem_limit_bytes=40 << 20),
    )(sums, stats, value_absorb, output_weight)


def body(ctx, query_nope, query_rope, key_absorb, value_absorb, output_weight, latent_cache, page_owner):
    requests, heads_here, nope_size = query_nope.shape
    latent_size = key_absorb.shape[2]
    rope_size = query_rope.shape[1] // heads_here
    score_scale = (nope_size + rope_size) ** (-0.5)
    gathered = gather_queries(query_nope, query_rope, key_absorb, ctx)
    owners = jnp.where(page_owner < 0, requests, page_owner)
    sums, stats = attention(gathered, latent_cache, owners, requests, heads_here, latent_size, score_scale)
    return project(sums, stats, value_absorb, output_weight, ctx)


def solution(mesh):
    return jax.shard_map(
        functools.partial(body, mesh.shape["ctx"]),
        mesh=mesh,
        in_specs=(
            P("groups", ("ctx", "head"), None),
            P("groups", ("ctx", "head")),
            P(("ctx", "head"), None, None),
            P(("ctx", "head"), None, None),
            P(("ctx", "head"), None),
            P(("groups", "ctx"), None, None),
            P(("groups", "ctx")),
        ),
        out_specs=P("groups", ("ctx", "head")),
        check_vma=False,
    )
```

```python
import functools

import jax
import jax.numpy as jnp
from jax import lax
from jax.experimental import pallas as pl
from jax.experimental.pallas import tpu as pltpu
from jax.sharding import PartitionSpec as P

F32 = jnp.float32
BF16 = jnp.bfloat16


def dot_nt(a, b):
    return lax.dot_general(a, b, (((1,), (1,)), ((), ())), preferred_element_type=F32)


def attention_kernel(heads_here, group, score_scale, owner_hbm, q_ref, cache_ref, sum_ref, stat_ref,
                     owner_ref, owner_sem, pages, query, scores, peak, total, acc, sems):
    ctx = q_ref.shape[0]
    slots, heads, _ = acc.shape
    requests = slots - 1
    page_count, page_len, _ = pages.shape
    latent = acc.shape[2]
    chunks = sems.shape[0]
    chunk = page_count // chunks

    def fetch(i):
        window = pl.ds(i * chunk, chunk)
        return pltpu.make_async_copy(cache_ref.at[window], pages.at[window], sems.at[i])

    owner_load = pltpu.make_async_copy(owner_hbm, owner_ref, owner_sem)
    owner_load.start()
    for i in range(chunks):
        fetch(i).start()
    for r in range(requests):
        rows = [q_ref[c, r * heads_here:(r + 1) * heads_here, :].astype(F32) for c in range(ctx)]
        query[r] = jnp.concatenate(rows, axis=0).astype(BF16)
    peak[...] = jnp.full_like(peak, -1e30)
    total[...] = jnp.zeros_like(total)
    acc[...] = jnp.zeros_like(acc)
    owner_load.wait()

    def owner_of(page):
        owner = owner_ref[page]
        return jnp.where(owner < 0, requests, owner)

    def score_group(base):
        owners = [owner_of(base + j) for j in range(group)]
        for j in range(group):
            found = dot_nt(query[jnp.minimum(owners[j], requests - 1)], pages[base + j]) * score_scale
            scores[base + j] = found
            peak[owners[j]] = jnp.maximum(peak[owners[j]], found)

    @pl.loop(0, chunks)
    def _(i):
        fetch(i).wait()

        @pl.loop(0, chunk // group)
        def _(g):
            score_group(i * chunk + g * group)

    for r in range(slots):
        peak[r] = jnp.broadcast_to(jnp.max(peak[r], axis=1, keepdims=True), peak.shape[1:])

    @pl.loop(0, page_count // group)
    def _(g):
        base = g * group
        owners = [owner_of(base + j) for j in range(group)]
        weights = []
        for j in range(group):
            weight = jnp.exp(scores[base + j] - peak[owners[j]])
            total[owners[j]] = total[owners[j]] + weight
            weights.append(weight.astype(BF16))
        for j in range(group):
            acc[owners[j]] = acc[owners[j]] + jnp.dot(
                weights[j], pages[base + j, :, :latent], preferred_element_type=F32)

    lane = lax.broadcasted_iota(jnp.int32, (heads, stat_ref.shape[-1]), 1)
    top = jnp.zeros(lane.shape, F32)
    norm = jnp.zeros(lane.shape, F32)
    for r in range(requests):
        top = jnp.where(lane == r, jnp.max(peak[r], axis=1, keepdims=True), top)
        norm = jnp.where(lane == r, jnp.sum(total[r], axis=1, keepdims=True), norm)
    for c in range(ctx):
        rows = slice(c * heads_here, (c + 1) * heads_here)
        part = acc[:requests, rows, :]
        sum_ref[c % 2, c // 2] = part.reshape(requests * heads_here, latent).astype(BF16)
        stat_ref[c % 2, c // 2, 0] = top[rows]
        stat_ref[c % 2, c // 2, 1] = norm[rows]


def attention(gathered, cache, owners, requests, heads_here, latent, score_scale):
    ctx, _, entry = gathered.shape
    page_count, page_len, _ = cache.shape
    heads = ctx * heads_here
    sum_shape = (2, ctx // 2, requests * heads_here, latent)
    stat_shape = (2, ctx // 2, 2, heads_here, 128)
    chunks = next(n for n in (14, 8, 7, 4, 2, 1) if page_count % n == 0)
    group = next(n for n in (16, 8, 4, 2, 1) if (page_count // chunks) % n == 0)
    return pl.pallas_call(
        functools.partial(attention_kernel, heads_here, group, score_scale),
        in_specs=[
            pl.BlockSpec(memory_space=pltpu.HBM),
            pl.BlockSpec(memory_space=pltpu.VMEM),
            pl.BlockSpec(memory_space=pltpu.HBM),
        ],
        out_specs=[pl.BlockSpec(memory_space=pltpu.VMEM)] * 2,
        scratch_shapes=[
            pltpu.SMEM((page_count,), jnp.int32),
            pltpu.SemaphoreType.DMA,
            pltpu.VMEM((page_count, page_len, entry), BF16),
            pltpu.VMEM((requests, heads, entry), BF16),
            pltpu.VMEM((page_count, heads, page_len), F32),
            pltpu.VMEM((requests + 1, heads, page_len), F32),
            pltpu.VMEM((requests + 1, heads, page_len), F32),
            pltpu.VMEM((requests + 1, heads, latent), F32),
            pltpu.SemaphoreType.DMA((chunks,)),
        ],
        out_shape=[
            jax.ShapeDtypeStruct(sum_shape, BF16),
            jax.ShapeDtypeStruct(stat_shape, F32),
        ],
        compiler_params=pltpu.CompilerParams(vmem_limit_bytes=48 << 20),
    )(owners, gathered, cache)


def remote(src, dst, send_sem, recv_sem, where):
    return pltpu.make_async_remote_copy(
        src_ref=src, dst_ref=dst, send_sem=send_sem, recv_sem=recv_sem,
        device_id=where, device_id_type=pl.DeviceIdType.MESH)


def gather_kernel(nz, nope_hbm, rope_hbm, key_hbm, out_ref, nope_ref, rope_ref, key_ref, in_sems, wide, rows, mine,
                  y_send, y_recv, up_send, up_recv, down_send, down_recv):
    requests, heads_here, _ = nope_ref.shape
    latent = key_ref.shape[2]
    rope = rope_ref.shape[1] // heads_here
    me = lax.axis_index("ctx")
    z, y = me // 2, me % 2
    partner = {"ctx": z * 2 + 1 - y}
    above, below = {"ctx": me + 2}, {"ctx": me - 2}
    has_above, has_below = z + 1 < nz, z > 0
    loads = [
        pltpu.make_async_copy(src, dst, in_sems.at[i])
        for i, (src, dst) in enumerate(((nope_hbm, nope_ref), (rope_hbm, rope_ref), (key_hbm, key_ref)))
    ]
    for load in loads:
        load.start()

    barrier = pltpu.get_barrier_semaphore()
    pl.semaphore_signal(barrier, inc=1, device_id=partner, device_id_type=pl.DeviceIdType.MESH)

    @pl.when(has_above)
    def _():
        pl.semaphore_signal(barrier, inc=1, device_id=above, device_id_type=pl.DeviceIdType.MESH)

    @pl.when(has_below)
    def _():
        pl.semaphore_signal(barrier, inc=1, device_id=below, device_id_type=pl.DeviceIdType.MESH)

    for load in loads:
        load.wait()
    wide[...] = nope_ref[...].astype(F32)
    for h in range(heads_here):
        rows[:, h, :latent] = jnp.dot(wide[:, h, :].astype(BF16), key_ref[h], preferred_element_type=F32)
        rows[:, h, latent:] = rope_ref[:, h * rope:(h + 1) * rope].astype(F32)
    value = rows[...].reshape(requests * heads_here, latent + rope).astype(BF16)
    mine[...] = value
    out_ref[me] = value

    pl.semaphore_wait(barrier, 1 + has_above.astype(jnp.int32) + has_below.astype(jnp.int32))

    def across(origin, src):
        slot = out_ref.at[origin * 2 + y]
        return remote(slot if src is None else src, slot, y_send.at[origin], y_recv.at[origin], partner)

    def upward(step, src=None):
        slot = out_ref.at[me - 2 * step]
        return remote(slot if src is None else src, slot, up_send.at[step], up_recv.at[step], above)

    def downward(step, src=None):
        slot = out_ref.at[me + 2 * step]
        return remote(slot if src is None else src, slot, down_send.at[step], down_recv.at[step], below)

    def arrival(slot, sem):
        return remote(slot, slot, sem, sem, partner)

    @pl.when(has_above)
    def _():
        upward(0, mine).start()

    @pl.when(has_below)
    def _():
        downward(0, mine).start()

    across(z, mine).start()
    for step in range(nz - 1):
        @pl.when(z - 1 - step >= 0)
        def _():
            arrival(out_ref.at[me - 2 * (step + 1)], up_recv.at[step]).wait_recv()
            if step + 1 < nz - 1:
                @pl.when(has_above)
                def _():
                    upward(step + 1).start()
            across(z - 1 - step, None).start()

        @pl.when(z + 1 + step < nz)
        def _():
            arrival(out_ref.at[me + 2 * (step + 1)], down_recv.at[step]).wait_recv()
            if step + 1 < nz - 1:
                @pl.when(has_below)
                def _():
                    downward(step + 1).start()
            across(z + 1 + step, None).start()

    for origin in range(nz):
        across(origin, mine).wait_send()
        arrival(out_ref.at[origin * 2 + 1 - y], y_recv.at[origin]).wait_recv()
    for step in range(nz - 1):
        @pl.when(has_above & (z - step >= 0))
        def _():
            upward(step, mine).wait_send()

        @pl.when(has_below & (z + step < nz))
        def _():
            downward(step, mine).wait_send()


def gather_queries(query_nope, query_rope, key_absorb, ctx):
    requests, heads_here, nope = query_nope.shape
    entry = key_absorb.shape[2] + query_rope.shape[1] // heads_here
    nz = ctx // 2
    vmem = pl.BlockSpec(memory_space=pltpu.VMEM)
    dma = pltpu.SemaphoreType.DMA
    return pl.pallas_call(
        functools.partial(gather_kernel, nz),
        out_shape=jax.ShapeDtypeStruct((ctx, requests * heads_here, entry), BF16),
        in_specs=[pl.BlockSpec(memory_space=pltpu.HBM)] * 3,
        out_specs=vmem,
        scratch_shapes=[
            pltpu.VMEM(query_nope.shape, BF16),
            pltpu.VMEM(query_rope.shape, BF16),
            pltpu.VMEM(key_absorb.shape, BF16),
            dma((3,)),
            pltpu.VMEM(query_nope.shape, F32),
            pltpu.VMEM((requests, heads_here, entry), F32),
            pltpu.VMEM((requests * heads_here, entry), BF16),
            dma((nz,)), dma((nz,)), dma((nz,)), dma((nz,)), dma((nz,)), dma((nz,)),
        ],
        compiler_params=pltpu.CompilerParams(collective_id=0, has_side_effects=True, vmem_limit_bytes=16 << 20),
    )(query_nope, query_rope, key_absorb)


def project_kernel(ctx, sum_ref, stat_ref, value_hbm, weight_ref, out_ref,
                   weight, value_ref, value_sem, y_sum, y_stat, c_sum, c_stat, z_sum, z_stat, wide,
                   h_keep, h_out, h_in, p_out, p_in,
                   w_sem, ys_send, ys_recv, yt_send, yt_recv, zs_send, zs_recv, zt_send, zt_recv,
                   h_send, h_recv, p_send, p_recv):
    nz = ctx // 2
    requests, half = out_ref.shape
    block = 2 * half
    heads_here, latent, _ = value_ref.shape
    me, core = lax.axis_index("ctx"), lax.axis_index("head")
    z, y = me // 2, me % 2
    partner, twin = {"ctx": z * 2 + 1 - y}, {"head": 1 - core}

    barrier = pltpu.get_barrier_semaphore()
    for k in range(1, ctx):
        pl.semaphore_signal(barrier, inc=1, device_id={"ctx": (me + k) % ctx}, device_id_type=pl.DeviceIdType.MESH)
    pl.semaphore_signal(barrier, inc=1, device_id=twin, device_id_type=pl.DeviceIdType.MESH)
    load = pltpu.make_async_copy(weight_ref, weight, w_sem)
    value_load = pltpu.make_async_copy(value_hbm, value_ref, value_sem)
    value_load.start()
    load.start()
    pl.semaphore_wait(barrier, ctx)

    stat_copy = remote(stat_ref.at[1 - y], y_stat, yt_send, yt_recv, partner)
    stat_copy.start()
    y_copies = []
    for k in range(nz):
        target = (z + 1 + k) % nz
        copy = remote(sum_ref.at[1 - y, target], y_sum.at[k], ys_send.at[k], ys_recv.at[k], partner)
        copy.start()
        y_copies.append(copy)
    stat_copy.wait_recv()

    def spread(factor):
        return jnp.concatenate([factor[:, r:r + 1] for r in range(requests)], axis=0)

    z_copies = []
    for k in range(nz):
        target = (z + 1 + k) % nz
        top_a, norm_a = stat_ref[y, target, 0], stat_ref[y, target, 1]
        top_b, norm_b = y_stat[target, 0], y_stat[target, 1]
        top = jnp.maximum(top_a, top_b)
        keep_a, keep_b = jnp.exp(top_a - top), jnp.exp(top_b - top)
        norm = keep_a * norm_a + keep_b * norm_b
        rows_a, rows_b = spread(keep_a), spread(keep_b)
        y_copies[k].wait_recv()
        both = rows_a * sum_ref[y, target].astype(F32) + rows_b * y_sum[k].astype(F32)
        if k < nz - 1:
            c_sum[k] = both.astype(BF16)
            c_stat[k, 0] = top
            c_stat[k, 1] = norm
            there = {"ctx": target * 2 + y}
            for copy in (
                remote(c_stat.at[k], z_stat.at[k], zt_send.at[k], zt_recv.at[k], there),
                remote(c_sum.at[k], z_sum.at[k], zs_send.at[k], zs_recv.at[k], there),
            ):
                copy.start()
                z_copies.append(copy)
    for copy in z_copies[0::2]:
        copy.wait_recv()
    highest = top
    for k in range(nz - 1):
        highest = jnp.maximum(highest, z_stat[k, 0])
    keep = jnp.exp(top - highest)
    all_norm = keep * norm
    factors = []
    for k in range(nz - 1):
        factors.append(jnp.exp(z_stat[k, 0] - highest))
        all_norm = all_norm + factors[k] * z_stat[k, 1]
    safe = jnp.where(all_norm > 0, all_norm, 1.0)
    total = spread(keep / safe) * both
    for k in range(nz - 1):
        z_copies[2 * k + 1].wait_recv()
        total = total + spread(factors[k] / safe) * z_sum[k].astype(F32)
    wide[...] = total.reshape(requests, heads_here, latent)
    outs = []
    value_load.wait()
    for h in range(heads_here):
        outs.append(jnp.dot(wide[:, h, :].astype(BF16), value_ref[h], preferred_element_type=F32).astype(BF16))
    head_out = jnp.concatenate(outs, axis=1)
    load.wait()

    aligned = block % 128 == 0
    h_copies, p_copies = [], []

    def place(k):
        return (me + 1 + k) % ctx if aligned else k

    def forward(k):
        target = place(k)
        h_copies[k].wait_recv()
        merged = h_keep[k] + h_in[k]
        if aligned:
            p_out[k] = merged.astype(BF16)
            if k < ctx - 1:
                copy = remote(p_out.at[k], p_in.at[k], p_send.at[k], p_recv.at[k], {"ctx": target})
                copy.start()
                p_copies.append(copy)
        else:
            p_out[k] = merged.astype(BF16)

            @pl.when(target != me)
            def _():
                slot = (target - me + ctx - 1) % ctx
                remote(p_out.at[k], p_in.at[slot], p_send.at[slot], p_recv.at[slot], {"ctx": target}).start()

    for k in range(ctx):
        if aligned:
            columns = weight[:, pl.ds(pl.multiple_of(place(k) * block, 128), block)]
        else:
            columns = weight[:, k * block:(k + 1) * block]
        part = jnp.dot(head_out, columns, preferred_element_type=F32)
        low, high = part[:, :half], part[:, half:]
        h_keep[k] = jnp.where(core == 0, low, high)
        h_out[k] = jnp.where(core == 0, high, low)
        copy = remote(h_out.at[k], h_in.at[k], h_send.at[k], h_recv.at[k], twin)
        copy.start()
        h_copies.append(copy)
        if k > 0:
            forward(k - 1)
    forward(ctx - 1)
    if aligned:
        result = h_keep[ctx - 1] + h_in[ctx - 1]
    else:
        result = p_out[me].astype(F32)
    for k in range(ctx - 1):
        remote(p_out.at[k], p_in.at[k], p_send.at[k], p_recv.at[k], partner).wait_recv()
        result = result + p_in[k].astype(F32)
    out_ref[...] = result.astype(BF16)
    for k in range(ctx - 1):
        remote(p_out.at[k], p_in.at[k], p_send.at[k], p_recv.at[k], partner).wait_send()
    for copy in h_copies + z_copies + y_copies + [stat_copy]:
        copy.wait_send()


def project(sums, stats, value_absorb, output_weight, ctx):
    nz = ctx // 2
    _, _, rows, latent = sums.shape
    heads_here = value_absorb.shape[0]
    requests = rows // heads_here
    half = output_weight.shape[1] // (2 * ctx)
    vmem = pl.BlockSpec(memory_space=pltpu.VMEM)
    dma = pltpu.SemaphoreType.DMA
    stat_tail = stats.shape[2:]
    return pl.pallas_call(
        functools.partial(project_kernel, ctx),
        out_shape=jax.ShapeDtypeStruct((requests, half), BF16),
        in_specs=[vmem, vmem] + [pl.BlockSpec(memory_space=pltpu.HBM)] * 2,
        out_specs=vmem,
        scratch_shapes=[
            pltpu.VMEM(output_weight.shape, BF16),
            pltpu.VMEM(value_absorb.shape, BF16),
            dma,
            pltpu.VMEM((nz, rows, latent), BF16),
            pltpu.VMEM((nz,) + stat_tail, F32),
            pltpu.VMEM((nz - 1, rows, latent), BF16),
            pltpu.VMEM((nz - 1,) + stat_tail, F32),
            pltpu.VMEM((nz - 1, rows, latent), BF16),
            pltpu.VMEM((nz - 1,) + stat_tail, F32),
            pltpu.VMEM((requests, heads_here, latent), F32),
            pltpu.VMEM((ctx, requests, half), F32),
            pltpu.VMEM((ctx, requests, half), F32),
            pltpu.VMEM((ctx, requests, half), F32),
            pltpu.VMEM((ctx, requests, half), BF16),
            pltpu.VMEM((ctx - 1, requests, half), BF16),
            dma, dma((nz,)), dma((nz,)), dma, dma,
            dma((nz - 1,)), dma((nz - 1,)), dma((nz - 1,)), dma((nz - 1,)),
            dma((ctx,)), dma((ctx,)), dma((ctx - 1,)), dma((ctx - 1,)),
        ],
        compiler_params=pltpu.CompilerParams(collective_id=1, has_side_effects=True, vmem_limit_bytes=40 << 20),
    )(sums, stats, value_absorb, output_weight)


def body(ctx, query_nope, query_rope, key_absorb, value_absorb, output_weight, latent_cache, page_owner):
    requests, heads_here, nope_size = query_nope.shape
    latent_size = key_absorb.shape[2]
    rope_size = query_rope.shape[1] // heads_here
    score_scale = (nope_size + rope_size) ** (-0.5)
    query_nope, query_rope, key_absorb, page_owner = (
        pltpu.with_memory_space_constraint(x, pltpu.HBM) for x in (query_nope, query_rope, key_absorb, page_owner))
    gathered = gather_queries(query_nope, query_rope, key_absorb, ctx)
    sums, stats = attention(gathered, latent_cache, page_owner, requests, heads_here, latent_size, score_scale)
    return project(sums, stats, value_absorb, output_weight, ctx)


def solution(mesh):
    return jax.shard_map(
        functools.partial(body, mesh.shape["ctx"]),
        mesh=mesh,
        in_specs=(
            P("groups", ("ctx", "head"), None),
            P("groups", ("ctx", "head")),
            P(("ctx", "head"), None, None),
            P(("ctx", "head"), None, None),
            P(("ctx", "head"), None),
            P(("groups", "ctx"), None, None),
            P(("groups", "ctx")),
        ),
        out_specs=P("groups", ("ctx", "head")),
        check_vma=False,
    )
```

```python
import functools

import jax
import jax.numpy as jnp
from jax import lax
from jax.experimental import pallas as pl
from jax.experimental.pallas import tpu as pltpu
from jax.sharding import PartitionSpec as P

PARTS = 2
F32 = jnp.float32
BF16 = jnp.bfloat16


def dot_nt(a, b):
    return lax.dot_general(a, b, (((1,), (1,)), ((), ())), preferred_element_type=F32)


def attention_kernel(heads_here, group, score_scale, owner_hbm, q_ref, cache_ref, sum_ref, stat_ref,
                     owner_ref, owner_sem, pages, query, scores, peak, total, acc, sems):
    ctx = q_ref.shape[0]
    slots, heads, _ = acc.shape
    requests = slots - 1
    page_count, page_len, _ = pages.shape
    latent = acc.shape[2]
    chunks = sems.shape[0]
    chunk = page_count // chunks

    def fetch(i):
        window = pl.ds(i * chunk, chunk)
        return pltpu.make_async_copy(cache_ref.at[window], pages.at[window], sems.at[i])

    owner_load = pltpu.make_async_copy(owner_hbm, owner_ref, owner_sem)
    owner_load.start()
    for i in range(chunks):
        fetch(i).start()
    for r in range(requests):
        rows = [q_ref[c, r * heads_here:(r + 1) * heads_here, :].astype(F32) for c in range(ctx)]
        query[r] = jnp.concatenate(rows, axis=0).astype(BF16)
    peak[...] = jnp.full_like(peak, -1e30)
    total[...] = jnp.zeros_like(total)
    acc[...] = jnp.zeros_like(acc)
    owner_load.wait()

    def owner_of(page):
        owner = owner_ref[page]
        return jnp.where(owner < 0, requests, owner)

    def score_group(base):
        owners = [owner_of(base + j) for j in range(group)]
        for j in range(group):
            found = dot_nt(query[jnp.minimum(owners[j], requests - 1)], pages[base + j]) * score_scale
            scores[base + j] = found
            peak[owners[j]] = jnp.maximum(peak[owners[j]], found)

    @pl.loop(0, chunks)
    def _(i):
        fetch(i).wait()

        @pl.loop(0, chunk // group)
        def _(g):
            score_group(i * chunk + g * group)

    for r in range(slots):
        peak[r] = jnp.broadcast_to(jnp.max(peak[r], axis=1, keepdims=True), peak.shape[1:])

    @pl.loop(0, page_count // group)
    def _(g):
        base = g * group
        owners = [owner_of(base + j) for j in range(group)]
        weights = []
        for j in range(group):
            weight = jnp.exp(scores[base + j] - peak[owners[j]])
            total[owners[j]] = total[owners[j]] + weight
            weights.append(weight.astype(BF16))
        for j in range(group):
            acc[owners[j]] = acc[owners[j]] + jnp.dot(
                weights[j], pages[base + j, :, :latent], preferred_element_type=F32)

    lane = lax.broadcasted_iota(jnp.int32, (heads, stat_ref.shape[-1]), 1)
    top = jnp.zeros(lane.shape, F32)
    norm = jnp.zeros(lane.shape, F32)
    for r in range(requests):
        top = jnp.where(lane == r, jnp.max(peak[r], axis=1, keepdims=True), top)
        norm = jnp.where(lane == r, jnp.sum(total[r], axis=1, keepdims=True), norm)
    for c in range(ctx):
        rows = slice(c * heads_here, (c + 1) * heads_here)
        part = acc[:requests, rows, :]
        sum_ref[c % 2, c // 2] = part.reshape(requests * heads_here, latent).astype(BF16)
        stat_ref[c % 2, c // 2, 0] = top[rows]
        stat_ref[c % 2, c // 2, 1] = norm[rows]


def attention(gathered, cache, owners, requests, heads_here, latent, score_scale):
    ctx, _, entry = gathered.shape
    page_count, page_len, _ = cache.shape
    heads = ctx * heads_here
    sum_shape = (2, ctx // 2, requests * heads_here, latent)
    stat_shape = (2, ctx // 2, 2, heads_here, 128)
    chunks = next(n for n in (14, 8, 7, 4, 2, 1) if page_count % n == 0)
    group = next(n for n in (16, 8, 4, 2, 1) if (page_count // chunks) % n == 0)
    return pl.pallas_call(
        functools.partial(attention_kernel, heads_here, group, score_scale),
        in_specs=[
            pl.BlockSpec(memory_space=pltpu.HBM),
            pl.BlockSpec(memory_space=pltpu.VMEM),
            pl.BlockSpec(memory_space=pltpu.HBM),
        ],
        out_specs=[pl.BlockSpec(memory_space=pltpu.VMEM)] * 2,
        scratch_shapes=[
            pltpu.SMEM((page_count,), jnp.int32),
            pltpu.SemaphoreType.DMA,
            pltpu.VMEM((page_count, page_len, entry), BF16),
            pltpu.VMEM((requests, heads, entry), BF16),
            pltpu.VMEM((page_count, heads, page_len), F32),
            pltpu.VMEM((requests + 1, heads, page_len), F32),
            pltpu.VMEM((requests + 1, heads, page_len), F32),
            pltpu.VMEM((requests + 1, heads, latent), F32),
            pltpu.SemaphoreType.DMA((chunks,)),
        ],
        out_shape=[
            jax.ShapeDtypeStruct(sum_shape, BF16),
            jax.ShapeDtypeStruct(stat_shape, F32),
        ],
        compiler_params=pltpu.CompilerParams(vmem_limit_bytes=48 << 20),
    )(owners, gathered, cache)


def remote(src, dst, send_sem, recv_sem, where):
    return pltpu.make_async_remote_copy(
        src_ref=src, dst_ref=dst, send_sem=send_sem, recv_sem=recv_sem,
        device_id=where, device_id_type=pl.DeviceIdType.MESH)


def gather_kernel(nz, nope_hbm, rope_hbm, key_hbm, out_ref, nope_ref, rope_ref, key_ref, in_sems, wide, rows, mine,
                  y_send, y_recv, up_send, up_recv, down_send, down_recv):
    requests, heads_here, _ = nope_ref.shape
    latent = key_ref.shape[2]
    rope = rope_ref.shape[1] // heads_here
    me = lax.axis_index("ctx")
    z, y = me // 2, me % 2
    partner = {"ctx": z * 2 + 1 - y}
    above, below = {"ctx": me + 2}, {"ctx": me - 2}
    has_above, has_below = z + 1 < nz, z > 0
    loads = [
        pltpu.make_async_copy(src, dst, in_sems.at[i])
        for i, (src, dst) in enumerate(((nope_hbm, nope_ref), (rope_hbm, rope_ref), (key_hbm, key_ref)))
    ]
    for load in loads:
        load.start()

    barrier = pltpu.get_barrier_semaphore()
    pl.semaphore_signal(barrier, inc=1, device_id=partner, device_id_type=pl.DeviceIdType.MESH)

    @pl.when(has_above)
    def _():
        pl.semaphore_signal(barrier, inc=1, device_id=above, device_id_type=pl.DeviceIdType.MESH)

    @pl.when(has_below)
    def _():
        pl.semaphore_signal(barrier, inc=1, device_id=below, device_id_type=pl.DeviceIdType.MESH)

    for load in loads:
        load.wait()
    wide[...] = nope_ref[...].astype(F32)
    for h in range(heads_here):
        rows[:, h, :latent] = jnp.dot(wide[:, h, :].astype(BF16), key_ref[h], preferred_element_type=F32)
        rows[:, h, latent:] = rope_ref[:, h * rope:(h + 1) * rope].astype(F32)
    value = rows[...].reshape(requests * heads_here, latent + rope).astype(BF16)
    mine[...] = value
    out_ref[me] = value

    pl.semaphore_wait(barrier, 1 + has_above.astype(jnp.int32) + has_below.astype(jnp.int32))

    depth = mine.shape[0] // PARTS

    def block(ref, part):
        return ref.at[part * depth:(part + 1) * depth]

    def across(origin, part, src=None):
        slot, i = block(out_ref.at[origin * 2 + y], part), origin * PARTS + part
        return remote(slot if src is None else block(src, part), slot, y_send.at[i], y_recv.at[i], partner)

    def upward(step, part, src=None):
        slot, i = block(out_ref.at[me - 2 * step], part), step * PARTS + part
        return remote(slot if src is None else block(src, part), slot, up_send.at[i], up_recv.at[i], above)

    def downward(step, part, src=None):
        slot, i = block(out_ref.at[me + 2 * step], part), step * PARTS + part
        return remote(slot if src is None else block(src, part), slot, down_send.at[i], down_recv.at[i], below)

    def arrival(row, part, sem):
        slot = block(out_ref.at[row], part)
        return remote(slot, slot, sem, sem, partner)

    for part in range(PARTS):
        @pl.when(has_above)
        def _():
            upward(0, part, mine).start()

        @pl.when(has_below)
        def _():
            downward(0, part, mine).start()

        across(z, part, mine).start()
    for step in range(nz - 1):
        for part in range(PARTS):
            @pl.when(z - 1 - step >= 0)
            def _():
                arrival(me - 2 * (step + 1), part, up_recv.at[step * PARTS + part]).wait_recv()
                if step + 1 < nz - 1:
                    @pl.when(has_above)
                    def _():
                        upward(step + 1, part).start()
                across(z - 1 - step, part).start()

            @pl.when(z + 1 + step < nz)
            def _():
                arrival(me + 2 * (step + 1), part, down_recv.at[step * PARTS + part]).wait_recv()
                if step + 1 < nz - 1:
                    @pl.when(has_below)
                    def _():
                        downward(step + 1, part).start()
                across(z + 1 + step, part).start()

    for part in range(PARTS):
        for origin in range(nz):
            across(origin, part, mine).wait_send()
            arrival(origin * 2 + 1 - y, part, y_recv.at[origin * PARTS + part]).wait_recv()
        for step in range(nz - 1):
            @pl.when(has_above & (z - step >= 0))
            def _():
                upward(step, part, mine).wait_send()

            @pl.when(has_below & (z + step < nz))
            def _():
                downward(step, part, mine).wait_send()


def gather_queries(query_nope, query_rope, key_absorb, ctx):
    requests, heads_here, nope = query_nope.shape
    entry = key_absorb.shape[2] + query_rope.shape[1] // heads_here
    nz = ctx // 2
    vmem = pl.BlockSpec(memory_space=pltpu.VMEM)
    dma = pltpu.SemaphoreType.DMA
    return pl.pallas_call(
        functools.partial(gather_kernel, nz),
        out_shape=jax.ShapeDtypeStruct((ctx, requests * heads_here, entry), BF16),
        in_specs=[pl.BlockSpec(memory_space=pltpu.HBM)] * 3,
        out_specs=vmem,
        scratch_shapes=[
            pltpu.VMEM(query_nope.shape, BF16),
            pltpu.VMEM(query_rope.shape, BF16),
            pltpu.VMEM(key_absorb.shape, BF16),
            dma((3,)),
            pltpu.VMEM(query_nope.shape, F32),
            pltpu.VMEM((requests, heads_here, entry), F32),
            pltpu.VMEM((requests * heads_here, entry), BF16),
            dma((nz * PARTS,)), dma((nz * PARTS,)), dma((nz * PARTS,)),
            dma((nz * PARTS,)), dma((nz * PARTS,)), dma((nz * PARTS,)),
        ],
        compiler_params=pltpu.CompilerParams(collective_id=0, has_side_effects=True, vmem_limit_bytes=16 << 20),
    )(query_nope, query_rope, key_absorb)


def project_kernel(ctx, sum_ref, stat_ref, value_hbm, weight_ref, out_ref,
                   weight, value_ref, value_sem, y_sum, y_stat, c_sum, c_stat, z_sum, z_stat, wide,
                   h_keep, h_out, h_in, p_out, p_in,
                   w_sem, ys_send, ys_recv, yt_send, yt_recv, zs_send, zs_recv, zt_send, zt_recv,
                   h_send, h_recv, p_send, p_recv):
    nz = ctx // 2
    requests, half = out_ref.shape
    block = 2 * half
    heads_here, latent, _ = value_ref.shape
    me, core = lax.axis_index("ctx"), lax.axis_index("head")
    z, y = me // 2, me % 2
    partner, twin = {"ctx": z * 2 + 1 - y}, {"head": 1 - core}

    barrier = pltpu.get_barrier_semaphore()
    for k in range(1, ctx):
        pl.semaphore_signal(barrier, inc=1, device_id={"ctx": (me + k) % ctx}, device_id_type=pl.DeviceIdType.MESH)
    pl.semaphore_signal(barrier, inc=1, device_id=twin, device_id_type=pl.DeviceIdType.MESH)
    load = pltpu.make_async_copy(weight_ref, weight, w_sem)
    value_load = pltpu.make_async_copy(value_hbm, value_ref, value_sem)
    value_load.start()
    load.start()
    pl.semaphore_wait(barrier, ctx)

    depth = y_sum.shape[1] // PARTS

    def lines(part):
        return slice(part * depth, (part + 1) * depth)

    stat_copy = remote(stat_ref.at[1 - y], y_stat, yt_send, yt_recv, partner)
    stat_copy.start()
    y_copies = []
    for k in range(nz):
        target = (z + 1 + k) % nz
        for part in range(PARTS):
            i = k * PARTS + part
            copy = remote(sum_ref.at[1 - y, target, lines(part)], y_sum.at[k, lines(part)],
                          ys_send.at[i], ys_recv.at[i], partner)
            copy.start()
            y_copies.append(copy)
    stat_copy.wait_recv()

    def spread(factor):
        return jnp.concatenate([factor[:, r:r + 1] for r in range(requests)], axis=0)

    z_copies, z_stats = [], []
    for k in range(nz):
        target = (z + 1 + k) % nz
        top_a, norm_a = stat_ref[y, target, 0], stat_ref[y, target, 1]
        top_b, norm_b = y_stat[target, 0], y_stat[target, 1]
        top = jnp.maximum(top_a, top_b)
        keep_a, keep_b = jnp.exp(top_a - top), jnp.exp(top_b - top)
        norm = keep_a * norm_a + keep_b * norm_b
        rows_a, rows_b = spread(keep_a), spread(keep_b)
        there = {"ctx": target * 2 + y}
        if k < nz - 1:
            c_stat[k, 0] = top
            c_stat[k, 1] = norm
            copy = remote(c_stat.at[k], z_stat.at[k], zt_send.at[k], zt_recv.at[k], there)
            copy.start()
            z_stats.append(copy)
        both = []
        for part in range(PARTS):
            i = k * PARTS + part
            y_copies[i].wait_recv()
            both.append(rows_a[lines(part)] * sum_ref[y, target, lines(part)].astype(F32)
                        + rows_b[lines(part)] * y_sum[k, lines(part)].astype(F32))
            if k < nz - 1:
                c_sum[k, lines(part)] = both[part].astype(BF16)
                copy = remote(c_sum.at[k, lines(part)], z_sum.at[k, lines(part)], zs_send.at[i], zs_recv.at[i], there)
                copy.start()
                z_copies.append(copy)
    both = jnp.concatenate(both, axis=0)
    for copy in z_stats:
        copy.wait_recv()
    highest = top
    for k in range(nz - 1):
        highest = jnp.maximum(highest, z_stat[k, 0])
    keep = jnp.exp(top - highest)
    all_norm = keep * norm
    factors = []
    for k in range(nz - 1):
        factors.append(jnp.exp(z_stat[k, 0] - highest))
        all_norm = all_norm + factors[k] * z_stat[k, 1]
    safe = jnp.where(all_norm > 0, all_norm, 1.0)
    total = spread(keep / safe) * both
    for k in range(nz - 1):
        for part in range(PARTS):
            z_copies[k * PARTS + part].wait_recv()
        total = total + spread(factors[k] / safe) * z_sum[k].astype(F32)
    wide[...] = total.reshape(requests, heads_here, latent)
    outs = []
    value_load.wait()
    for h in range(heads_here):
        outs.append(jnp.dot(wide[:, h, :].astype(BF16), value_ref[h], preferred_element_type=F32).astype(BF16))
    head_out = jnp.concatenate(outs, axis=1)
    load.wait()

    aligned = block % 128 == 0
    h_copies, p_copies = [], []

    def place(k):
        return (me + 1 + k) % ctx if aligned else k

    def forward(k):
        target = place(k)
        h_copies[k].wait_recv()
        merged = h_keep[k] + h_in[k]
        if aligned:
            p_out[k] = merged.astype(BF16)
            if k < ctx - 1:
                copy = remote(p_out.at[k], p_in.at[k], p_send.at[k], p_recv.at[k], {"ctx": target})
                copy.start()
                p_copies.append(copy)
        else:
            p_out[k] = merged.astype(BF16)

            @pl.when(target != me)
            def _():
                slot = (target - me + ctx - 1) % ctx
                remote(p_out.at[k], p_in.at[slot], p_send.at[slot], p_recv.at[slot], {"ctx": target}).start()

    for k in range(ctx):
        if aligned:
            columns = weight[:, pl.ds(pl.multiple_of(place(k) * block, 128), block)]
        else:
            columns = weight[:, k * block:(k + 1) * block]
        part = jnp.dot(head_out, columns, preferred_element_type=F32)
        low, high = part[:, :half], part[:, half:]
        h_keep[k] = jnp.where(core == 0, low, high)
        h_out[k] = jnp.where(core == 0, high, low)
        copy = remote(h_out.at[k], h_in.at[k], h_send.at[k], h_recv.at[k], twin)
        copy.start()
        h_copies.append(copy)
        if k > 0:
            forward(k - 1)
    forward(ctx - 1)
    if aligned:
        result = h_keep[ctx - 1] + h_in[ctx - 1]
    else:
        result = p_out[me].astype(F32)
    for k in range(ctx - 1):
        remote(p_out.at[k], p_in.at[k], p_send.at[k], p_recv.at[k], partner).wait_recv()
        result = result + p_in[k].astype(F32)
    out_ref[...] = result.astype(BF16)
    for k in range(ctx - 1):
        remote(p_out.at[k], p_in.at[k], p_send.at[k], p_recv.at[k], partner).wait_send()
    for copy in h_copies + z_copies + z_stats + y_copies + [stat_copy]:
        copy.wait_send()


def project(sums, stats, value_absorb, output_weight, ctx):
    nz = ctx // 2
    _, _, rows, latent = sums.shape
    heads_here = value_absorb.shape[0]
    requests = rows // heads_here
    half = output_weight.shape[1] // (2 * ctx)
    vmem = pl.BlockSpec(memory_space=pltpu.VMEM)
    dma = pltpu.SemaphoreType.DMA
    stat_tail = stats.shape[2:]
    return pl.pallas_call(
        functools.partial(project_kernel, ctx),
        out_shape=jax.ShapeDtypeStruct((requests, half), BF16),
        in_specs=[vmem, vmem] + [pl.BlockSpec(memory_space=pltpu.HBM)] * 2,
        out_specs=vmem,
        scratch_shapes=[
            pltpu.VMEM(output_weight.shape, BF16),
            pltpu.VMEM(value_absorb.shape, BF16),
            dma,
            pltpu.VMEM((nz, rows, latent), BF16),
            pltpu.VMEM((nz,) + stat_tail, F32),
            pltpu.VMEM((nz - 1, rows, latent), BF16),
            pltpu.VMEM((nz - 1,) + stat_tail, F32),
            pltpu.VMEM((nz - 1, rows, latent), BF16),
            pltpu.VMEM((nz - 1,) + stat_tail, F32),
            pltpu.VMEM((requests, heads_here, latent), F32),
            pltpu.VMEM((ctx, requests, half), F32),
            pltpu.VMEM((ctx, requests, half), F32),
            pltpu.VMEM((ctx, requests, half), F32),
            pltpu.VMEM((ctx, requests, half), BF16),
            pltpu.VMEM((ctx - 1, requests, half), BF16),
            dma, dma((nz * PARTS,)), dma((nz * PARTS,)), dma, dma,
            dma(((nz - 1) * PARTS,)), dma(((nz - 1) * PARTS,)), dma((nz - 1,)), dma((nz - 1,)),
            dma((ctx,)), dma((ctx,)), dma((ctx - 1,)), dma((ctx - 1,)),
        ],
        compiler_params=pltpu.CompilerParams(collective_id=1, has_side_effects=True, vmem_limit_bytes=40 << 20),
    )(sums, stats, value_absorb, output_weight)


def body(ctx, query_nope, query_rope, key_absorb, value_absorb, output_weight, latent_cache, page_owner):
    requests, heads_here, nope_size = query_nope.shape
    latent_size = key_absorb.shape[2]
    rope_size = query_rope.shape[1] // heads_here
    score_scale = (nope_size + rope_size) ** (-0.5)
    query_nope, query_rope, key_absorb, page_owner = (
        pltpu.with_memory_space_constraint(x, pltpu.HBM) for x in (query_nope, query_rope, key_absorb, page_owner))
    gathered = gather_queries(query_nope, query_rope, key_absorb, ctx)
    sums, stats = attention(gathered, latent_cache, page_owner, requests, heads_here, latent_size, score_scale)
    return project(sums, stats, value_absorb, output_weight, ctx)


def solution(mesh):
    return jax.shard_map(
        functools.partial(body, mesh.shape["ctx"]),
        mesh=mesh,
        in_specs=(
            P("groups", ("ctx", "head"), None),
            P("groups", ("ctx", "head")),
            P(("ctx", "head"), None, None),
            P(("ctx", "head"), None, None),
            P(("ctx", "head"), None),
            P(("groups", "ctx"), None, None),
            P(("groups", "ctx")),
        ),
        out_specs=P("groups", ("ctx", "head")),
        check_vma=False,
    )
```

```python
import functools

import jax
import jax.numpy as jnp
from jax import lax
from jax.experimental import pallas as pl
from jax.experimental.pallas import tpu as pltpu
from jax.sharding import PartitionSpec as P

PARTS = 4
F32 = jnp.float32
BF16 = jnp.bfloat16


def dot_nt(a, b):
    return lax.dot_general(a, b, (((1,), (1,)), ((), ())), preferred_element_type=F32)


def attention_kernel(heads_here, group, score_scale, owner_hbm, q_ref, cache_ref, sum_ref, stat_ref,
                     owner_ref, owner_sem, pages, query, scores, peak, total, acc, sems):
    ctx = q_ref.shape[0]
    slots, heads, _ = acc.shape
    requests = slots - 1
    page_count, page_len, _ = pages.shape
    latent = acc.shape[2]
    chunks = sems.shape[0]
    chunk = page_count // chunks

    def fetch(i):
        window = pl.ds(i * chunk, chunk)
        return pltpu.make_async_copy(cache_ref.at[window], pages.at[window], sems.at[i])

    owner_load = pltpu.make_async_copy(owner_hbm, owner_ref, owner_sem)
    owner_load.start()
    for i in range(chunks):
        fetch(i).start()
    for r in range(requests):
        rows = [q_ref[c, r * heads_here:(r + 1) * heads_here, :].astype(F32) for c in range(ctx)]
        query[r] = jnp.concatenate(rows, axis=0).astype(BF16)
    peak[...] = jnp.full_like(peak, -1e30)
    total[...] = jnp.zeros_like(total)
    acc[...] = jnp.zeros_like(acc)
    owner_load.wait()

    def owner_of(page):
        owner = owner_ref[page]
        return jnp.where(owner < 0, requests, owner)

    def score_group(base):
        owners = [owner_of(base + j) for j in range(group)]
        for j in range(group):
            found = dot_nt(query[jnp.minimum(owners[j], requests - 1)], pages[base + j]) * score_scale
            scores[base + j] = found
            peak[owners[j]] = jnp.maximum(peak[owners[j]], found)

    @pl.loop(0, chunks)
    def _(i):
        fetch(i).wait()

        @pl.loop(0, chunk // group)
        def _(g):
            score_group(i * chunk + g * group)

    for r in range(slots):
        peak[r] = jnp.broadcast_to(jnp.max(peak[r], axis=1, keepdims=True), peak.shape[1:])

    @pl.loop(0, page_count // group)
    def _(g):
        base = g * group
        owners = [owner_of(base + j) for j in range(group)]
        weights = []
        for j in range(group):
            weight = jnp.exp(scores[base + j] - peak[owners[j]])
            total[owners[j]] = total[owners[j]] + weight
            weights.append(weight.astype(BF16))
        for j in range(group):
            acc[owners[j]] = acc[owners[j]] + jnp.dot(
                weights[j], pages[base + j, :, :latent], preferred_element_type=F32)

    lane = lax.broadcasted_iota(jnp.int32, (heads, stat_ref.shape[-1]), 1)
    top = jnp.zeros(lane.shape, F32)
    norm = jnp.zeros(lane.shape, F32)
    for r in range(requests):
        top = jnp.where(lane == r, jnp.max(peak[r], axis=1, keepdims=True), top)
        norm = jnp.where(lane == r, jnp.sum(total[r], axis=1, keepdims=True), norm)
    for c in range(ctx):
        rows = slice(c * heads_here, (c + 1) * heads_here)
        part = acc[:requests, rows, :]
        sum_ref[c % 2, c // 2] = part.reshape(requests * heads_here, latent).astype(BF16)
        stat_ref[c % 2, c // 2, 0] = top[rows]
        stat_ref[c % 2, c // 2, 1] = norm[rows]


def attention(gathered, cache, owners, requests, heads_here, latent, score_scale):
    ctx, _, entry = gathered.shape
    page_count, page_len, _ = cache.shape
    heads = ctx * heads_here
    sum_shape = (2, ctx // 2, requests * heads_here, latent)
    stat_shape = (2, ctx // 2, 2, heads_here, 128)
    chunks = next(n for n in (14, 8, 7, 4, 2, 1) if page_count % n == 0)
    group = next(n for n in (16, 8, 4, 2, 1) if (page_count // chunks) % n == 0)
    return pl.pallas_call(
        functools.partial(attention_kernel, heads_here, group, score_scale),
        in_specs=[
            pl.BlockSpec(memory_space=pltpu.HBM),
            pl.BlockSpec(memory_space=pltpu.VMEM),
            pl.BlockSpec(memory_space=pltpu.HBM),
        ],
        out_specs=[pl.BlockSpec(memory_space=pltpu.VMEM)] * 2,
        scratch_shapes=[
            pltpu.SMEM((page_count,), jnp.int32),
            pltpu.SemaphoreType.DMA,
            pltpu.VMEM((page_count, page_len, entry), BF16),
            pltpu.VMEM((requests, heads, entry), BF16),
            pltpu.VMEM((page_count, heads, page_len), F32),
            pltpu.VMEM((requests + 1, heads, page_len), F32),
            pltpu.VMEM((requests + 1, heads, page_len), F32),
            pltpu.VMEM((requests + 1, heads, latent), F32),
            pltpu.SemaphoreType.DMA((chunks,)),
        ],
        out_shape=[
            jax.ShapeDtypeStruct(sum_shape, BF16),
            jax.ShapeDtypeStruct(stat_shape, F32),
        ],
        compiler_params=pltpu.CompilerParams(vmem_limit_bytes=48 << 20),
    )(owners, gathered, cache)


def remote(src, dst, send_sem, recv_sem, where):
    return pltpu.make_async_remote_copy(
        src_ref=src, dst_ref=dst, send_sem=send_sem, recv_sem=recv_sem,
        device_id=where, device_id_type=pl.DeviceIdType.MESH)


def gather_kernel(nz, nope_hbm, rope_hbm, key_hbm, out_ref, nope_ref, rope_ref, key_ref, in_sems, wide, rows, mine,
                  y_send, y_recv, up_send, up_recv, down_send, down_recv):
    requests, heads_here, _ = nope_ref.shape
    latent = key_ref.shape[2]
    rope = rope_ref.shape[1] // heads_here
    me = lax.axis_index("ctx")
    z, y = me // 2, me % 2
    partner = {"ctx": z * 2 + 1 - y}
    above, below = {"ctx": me + 2}, {"ctx": me - 2}
    has_above, has_below = z + 1 < nz, z > 0
    loads = [
        pltpu.make_async_copy(src, dst, in_sems.at[i])
        for i, (src, dst) in enumerate(((nope_hbm, nope_ref), (rope_hbm, rope_ref), (key_hbm, key_ref)))
    ]
    for load in loads:
        load.start()

    barrier = pltpu.get_barrier_semaphore()
    pl.semaphore_signal(barrier, inc=1, device_id=partner, device_id_type=pl.DeviceIdType.MESH)

    @pl.when(has_above)
    def _():
        pl.semaphore_signal(barrier, inc=1, device_id=above, device_id_type=pl.DeviceIdType.MESH)

    @pl.when(has_below)
    def _():
        pl.semaphore_signal(barrier, inc=1, device_id=below, device_id_type=pl.DeviceIdType.MESH)

    for load in loads:
        load.wait()
    wide[...] = nope_ref[...].astype(F32)
    for h in range(heads_here):
        rows[:, h, :latent] = jnp.dot(wide[:, h, :].astype(BF16), key_ref[h], preferred_element_type=F32)
        rows[:, h, latent:] = rope_ref[:, h * rope:(h + 1) * rope].astype(F32)
    value = rows[...].reshape(requests * heads_here, latent + rope).astype(BF16)
    mine[...] = value
    out_ref[me] = value

    pl.semaphore_wait(barrier, 1 + has_above.astype(jnp.int32) + has_below.astype(jnp.int32))

    depth = mine.shape[0] // PARTS

    def block(ref, part):
        return ref.at[part * depth:(part + 1) * depth]

    def across(origin, part, src=None):
        slot, i = block(out_ref.at[origin * 2 + y], part), origin * PARTS + part
        return remote(slot if src is None else block(src, part), slot, y_send.at[i], y_recv.at[i], partner)

    def upward(step, part, src=None):
        slot, i = block(out_ref.at[me - 2 * step], part), step * PARTS + part
        return remote(slot if src is None else block(src, part), slot, up_send.at[i], up_recv.at[i], above)

    def downward(step, part, src=None):
        slot, i = block(out_ref.at[me + 2 * step], part), step * PARTS + part
        return remote(slot if src is None else block(src, part), slot, down_send.at[i], down_recv.at[i], below)

    def arrival(row, part, sem):
        slot = block(out_ref.at[row], part)
        return remote(slot, slot, sem, sem, partner)

    for part in range(PARTS):
        @pl.when(has_above)
        def _():
            upward(0, part, mine).start()

        @pl.when(has_below)
        def _():
            downward(0, part, mine).start()

        across(z, part, mine).start()
    for step in range(nz - 1):
        for part in range(PARTS):
            @pl.when(z - 1 - step >= 0)
            def _():
                arrival(me - 2 * (step + 1), part, up_recv.at[step * PARTS + part]).wait_recv()
                if step + 1 < nz - 1:
                    @pl.when(has_above)
                    def _():
                        upward(step + 1, part).start()
                across(z - 1 - step, part).start()

            @pl.when(z + 1 + step < nz)
            def _():
                arrival(me + 2 * (step + 1), part, down_recv.at[step * PARTS + part]).wait_recv()
                if step + 1 < nz - 1:
                    @pl.when(has_below)
                    def _():
                        downward(step + 1, part).start()
                across(z + 1 + step, part).start()

    for part in range(PARTS):
        for origin in range(nz):
            across(origin, part, mine).wait_send()
            arrival(origin * 2 + 1 - y, part, y_recv.at[origin * PARTS + part]).wait_recv()
        for step in range(nz - 1):
            @pl.when(has_above & (z - step >= 0))
            def _():
                upward(step, part, mine).wait_send()

            @pl.when(has_below & (z + step < nz))
            def _():
                downward(step, part, mine).wait_send()


def gather_queries(query_nope, query_rope, key_absorb, ctx):
    requests, heads_here, nope = query_nope.shape
    entry = key_absorb.shape[2] + query_rope.shape[1] // heads_here
    nz = ctx // 2
    vmem = pl.BlockSpec(memory_space=pltpu.VMEM)
    dma = pltpu.SemaphoreType.DMA
    return pl.pallas_call(
        functools.partial(gather_kernel, nz),
        out_shape=jax.ShapeDtypeStruct((ctx, requests * heads_here, entry), BF16),
        in_specs=[pl.BlockSpec(memory_space=pltpu.HBM)] * 3,
        out_specs=vmem,
        scratch_shapes=[
            pltpu.VMEM(query_nope.shape, BF16),
            pltpu.VMEM(query_rope.shape, BF16),
            pltpu.VMEM(key_absorb.shape, BF16),
            dma((3,)),
            pltpu.VMEM(query_nope.shape, F32),
            pltpu.VMEM((requests, heads_here, entry), F32),
            pltpu.VMEM((requests * heads_here, entry), BF16),
            dma((nz * PARTS,)), dma((nz * PARTS,)), dma((nz * PARTS,)),
            dma((nz * PARTS,)), dma((nz * PARTS,)), dma((nz * PARTS,)),
        ],
        compiler_params=pltpu.CompilerParams(collective_id=0, has_side_effects=True, vmem_limit_bytes=16 << 20),
    )(query_nope, query_rope, key_absorb)


def project_kernel(ctx, sum_ref, stat_ref, value_hbm, weight_ref, out_ref,
                   weight, value_ref, value_sem, y_sum, y_stat, c_sum, c_stat, z_sum, z_stat, wide,
                   h_keep, h_out, h_in, p_out, p_in,
                   w_sem, ys_send, ys_recv, yt_send, yt_recv, zs_send, zs_recv, zt_send, zt_recv,
                   h_send, h_recv, p_send, p_recv):
    nz = ctx // 2
    requests, half = out_ref.shape
    block = 2 * half
    heads_here, latent, _ = value_ref.shape
    me, core = lax.axis_index("ctx"), lax.axis_index("head")
    z, y = me // 2, me % 2
    partner, twin = {"ctx": z * 2 + 1 - y}, {"head": 1 - core}

    barrier = pltpu.get_barrier_semaphore()
    for k in range(1, ctx):
        pl.semaphore_signal(barrier, inc=1, device_id={"ctx": (me + k) % ctx}, device_id_type=pl.DeviceIdType.MESH)
    pl.semaphore_signal(barrier, inc=1, device_id=twin, device_id_type=pl.DeviceIdType.MESH)
    load = pltpu.make_async_copy(weight_ref, weight, w_sem)
    value_load = pltpu.make_async_copy(value_hbm, value_ref, value_sem)
    value_load.start()
    load.start()
    pl.semaphore_wait(barrier, ctx)

    depth = y_sum.shape[1] // PARTS

    def lines(part):
        return slice(part * depth, (part + 1) * depth)

    stat_copy = remote(stat_ref.at[1 - y], y_stat, yt_send, yt_recv, partner)
    stat_copy.start()
    y_copies = []
    for k in range(nz):
        target = (z + 1 + k) % nz
        for part in range(PARTS):
            i = k * PARTS + part
            copy = remote(sum_ref.at[1 - y, target, lines(part)], y_sum.at[k, lines(part)],
                          ys_send.at[i], ys_recv.at[i], partner)
            copy.start()
            y_copies.append(copy)
    stat_copy.wait_recv()

    def spread(factor):
        return jnp.concatenate([factor[:, r:r + 1] for r in range(requests)], axis=0)

    z_copies, z_stats = [], []
    for k in range(nz):
        target = (z + 1 + k) % nz
        top_a, norm_a = stat_ref[y, target, 0], stat_ref[y, target, 1]
        top_b, norm_b = y_stat[target, 0], y_stat[target, 1]
        top = jnp.maximum(top_a, top_b)
        keep_a, keep_b = jnp.exp(top_a - top), jnp.exp(top_b - top)
        norm = keep_a * norm_a + keep_b * norm_b
        rows_a, rows_b = spread(keep_a), spread(keep_b)
        there = {"ctx": target * 2 + y}
        if k < nz - 1:
            c_stat[k, 0] = top
            c_stat[k, 1] = norm
            copy = remote(c_stat.at[k], z_stat.at[k], zt_send.at[k], zt_recv.at[k], there)
            copy.start()
            z_stats.append(copy)
        both = []
        for part in range(PARTS):
            i = k * PARTS + part
            y_copies[i].wait_recv()
            both.append(rows_a[lines(part)] * sum_ref[y, target, lines(part)].astype(F32)
                        + rows_b[lines(part)] * y_sum[k, lines(part)].astype(F32))
            if k < nz - 1:
                c_sum[k, lines(part)] = both[part].astype(BF16)
                copy = remote(c_sum.at[k, lines(part)], z_sum.at[k, lines(part)], zs_send.at[i], zs_recv.at[i], there)
                copy.start()
                z_copies.append(copy)
    both = jnp.concatenate(both, axis=0)
    for copy in z_stats:
        copy.wait_recv()
    highest = top
    for k in range(nz - 1):
        highest = jnp.maximum(highest, z_stat[k, 0])
    keep = jnp.exp(top - highest)
    all_norm = keep * norm
    factors = []
    for k in range(nz - 1):
        factors.append(jnp.exp(z_stat[k, 0] - highest))
        all_norm = all_norm + factors[k] * z_stat[k, 1]
    safe = jnp.where(all_norm > 0, all_norm, 1.0)
    total = spread(keep / safe) * both
    for k in range(nz - 1):
        for part in range(PARTS):
            z_copies[k * PARTS + part].wait_recv()
        total = total + spread(factors[k] / safe) * z_sum[k].astype(F32)
    wide[...] = total.reshape(requests, heads_here, latent)
    outs = []
    value_load.wait()
    for h in range(heads_here):
        outs.append(jnp.dot(wide[:, h, :].astype(BF16), value_ref[h], preferred_element_type=F32).astype(BF16))
    head_out = jnp.concatenate(outs, axis=1)
    load.wait()

    aligned = block % 128 == 0
    h_copies, p_copies = [], []

    def place(k):
        return (me + 1 + k) % ctx if aligned else k

    def forward(k):
        target = place(k)
        h_copies[k].wait_recv()
        merged = h_keep[k] + h_in[k]
        if aligned:
            p_out[k] = merged.astype(BF16)
            if k < ctx - 1:
                copy = remote(p_out.at[k], p_in.at[k], p_send.at[k], p_recv.at[k], {"ctx": target})
                copy.start()
                p_copies.append(copy)
        else:
            p_out[k] = merged.astype(BF16)

            @pl.when(target != me)
            def _():
                slot = (target - me + ctx - 1) % ctx
                remote(p_out.at[k], p_in.at[slot], p_send.at[slot], p_recv.at[slot], {"ctx": target}).start()

    for k in range(ctx):
        if aligned:
            columns = weight[:, pl.ds(pl.multiple_of(place(k) * block, 128), block)]
        else:
            columns = weight[:, k * block:(k + 1) * block]
        part = jnp.dot(head_out, columns, preferred_element_type=F32)
        low, high = part[:, :half], part[:, half:]
        h_keep[k] = jnp.where(core == 0, low, high)
        h_out[k] = jnp.where(core == 0, high, low)
        copy = remote(h_out.at[k], h_in.at[k], h_send.at[k], h_recv.at[k], twin)
        copy.start()
        h_copies.append(copy)
        if k > 0:
            forward(k - 1)
    forward(ctx - 1)
    if aligned:
        result = h_keep[ctx - 1] + h_in[ctx - 1]
    else:
        result = p_out[me].astype(F32)
    for k in range(ctx - 1):
        remote(p_out.at[k], p_in.at[k], p_send.at[k], p_recv.at[k], partner).wait_recv()
        result = result + p_in[k].astype(F32)
    out_ref[...] = result.astype(BF16)
    for k in range(ctx - 1):
        remote(p_out.at[k], p_in.at[k], p_send.at[k], p_recv.at[k], partner).wait_send()
    for copy in h_copies + z_copies + z_stats + y_copies + [stat_copy]:
        copy.wait_send()


def project(sums, stats, value_absorb, output_weight, ctx):
    nz = ctx // 2
    _, _, rows, latent = sums.shape
    heads_here = value_absorb.shape[0]
    requests = rows // heads_here
    half = output_weight.shape[1] // (2 * ctx)
    vmem = pl.BlockSpec(memory_space=pltpu.VMEM)
    dma = pltpu.SemaphoreType.DMA
    stat_tail = stats.shape[2:]
    return pl.pallas_call(
        functools.partial(project_kernel, ctx),
        out_shape=jax.ShapeDtypeStruct((requests, half), BF16),
        in_specs=[vmem, vmem] + [pl.BlockSpec(memory_space=pltpu.HBM)] * 2,
        out_specs=vmem,
        scratch_shapes=[
            pltpu.VMEM(output_weight.shape, BF16),
            pltpu.VMEM(value_absorb.shape, BF16),
            dma,
            pltpu.VMEM((nz, rows, latent), BF16),
            pltpu.VMEM((nz,) + stat_tail, F32),
            pltpu.VMEM((nz - 1, rows, latent), BF16),
            pltpu.VMEM((nz - 1,) + stat_tail, F32),
            pltpu.VMEM((nz - 1, rows, latent), BF16),
            pltpu.VMEM((nz - 1,) + stat_tail, F32),
            pltpu.VMEM((requests, heads_here, latent), F32),
            pltpu.VMEM((ctx, requests, half), F32),
            pltpu.VMEM((ctx, requests, half), F32),
            pltpu.VMEM((ctx, requests, half), F32),
            pltpu.VMEM((ctx, requests, half), BF16),
            pltpu.VMEM((ctx - 1, requests, half), BF16),
            dma, dma((nz * PARTS,)), dma((nz * PARTS,)), dma, dma,
            dma(((nz - 1) * PARTS,)), dma(((nz - 1) * PARTS,)), dma((nz - 1,)), dma((nz - 1,)),
            dma((ctx,)), dma((ctx,)), dma((ctx - 1,)), dma((ctx - 1,)),
        ],
        compiler_params=pltpu.CompilerParams(collective_id=1, has_side_effects=True, vmem_limit_bytes=40 << 20),
    )(sums, stats, value_absorb, output_weight)


def body(ctx, query_nope, query_rope, key_absorb, value_absorb, output_weight, latent_cache, page_owner):
    requests, heads_here, nope_size = query_nope.shape
    latent_size = key_absorb.shape[2]
    rope_size = query_rope.shape[1] // heads_here
    score_scale = (nope_size + rope_size) ** (-0.5)
    query_nope, query_rope, key_absorb, page_owner = (
        pltpu.with_memory_space_constraint(x, pltpu.HBM) for x in (query_nope, query_rope, key_absorb, page_owner))
    gathered = gather_queries(query_nope, query_rope, key_absorb, ctx)
    sums, stats = attention(gathered, latent_cache, page_owner, requests, heads_here, latent_size, score_scale)
    return project(sums, stats, value_absorb, output_weight, ctx)


def solution(mesh):
    return jax.shard_map(
        functools.partial(body, mesh.shape["ctx"]),
        mesh=mesh,
        in_specs=(
            P("groups", ("ctx", "head"), None),
            P("groups", ("ctx", "head")),
            P(("ctx", "head"), None, None),
            P(("ctx", "head"), None, None),
            P(("ctx", "head"), None),
            P(("groups", "ctx"), None, None),
            P(("groups", "ctx")),
        ),
        out_specs=P("groups", ("ctx", "head")),
        check_vma=False,
    )
```
